512 devices in a mesh: dp: 8 (over x, core), expert: 64 (over y, z).
Axes of the slice: x: 4, y: 4, z: 16, core: 2. Of those that a mesh axis runs over, the one named last changes fastest.
Arguments:
- tokens: bfloat16 [8192, 2048], P('expert', 'dp'), may hold values from -6 to 6
- cotangent: bfloat16 [8192, 2048], P('expert', 'dp'), may hold values from -6 to 6
- routes: int32 [8192, 8], P('expert'), may hold values from 0 to 63, as said below
- mix_weights: float32 [8192, 8], P('expert'), may hold values from 0.05 to 0.5
- w_gate: bfloat16 [64, 2048, 384], P('expert', 'dp'), may hold values from -0.125 to 0.125
- w_up: bfloat16 [64, 2048, 384], P('expert', 'dp'), may hold values from -0.125 to 0.125
- w_down: bfloat16 [64, 384, 2048], P('expert', None, 'dp'), may hold values from -0.3125 to 0.3125
Outputs:
- mixed: bfloat16 [8192, 2048], P('expert', 'dp')
- token_grad: bfloat16 [8192, 2048], P('expert', 'dp')
- gate_grad: float32 [64, 2048, 384], P('expert', 'dp')
- up_grad: float32 [64, 2048, 384], P('expert', 'dp')
- down_grad: float32 [64, 384, 2048], P('expert', None, 'dp')
The draws below stay inside these ranges and needn't reach their ends.
Inputs may be any that keep to these rules, and one draw needn't show every extreme that they name: `routes`: each row names 8 different experts. In each aligned block of 128 rows at most 32 rows name the same expert, and some block reaches that. In all, at most 1792 rows name one expert, and some expert is named by exactly that many.
All inputs are finite; a program needn't handle non-finite values.
Results may differ from the reference program's by a relative error of at most 0.023.
Values may be sent and summed in bfloat16 or wider, within the bound.
A program may use at most 64 MiB of HBM per device.

```python
import math
import jax
import jax.numpy as jnp
from jax import lax

D = 2048
FF = 384
TOPK = 8
TOK_DEV = 128
EXPERTS = 64
TOKENS = 8192
DPART = 256
EXP_CAP = 1792
N_DP = 8


def draw_routes(key, part):
    sources = TOKENS // TOK_DEV
    experts_all = EXPERTS
    mean_count = TOK_DEV * TOPK // experts_all
    quarter = mean_count // 4
    key_list = jax.random.split(jax.random.fold_in(key, 11), 6)
    hot_expert = jax.random.randint(key_list[0], (), 0, experts_all)
    pair_count = sources // 2
    pair_ids = jnp.arange(pair_count, dtype=jnp.int32)
    spread_pair = jax.random.randint(key_list[1], (pair_count,), 0, quarter + 1)
    widest = jax.random.randint(key_list[2], (), 0, pair_count)
    spread_pair = jnp.where(pair_ids == widest, quarter, spread_pair)
    flip_sign = 2 * jax.random.randint(key_list[3], (pair_count,), 0, 2) - 1
    extra_rows = jnp.stack([flip_sign * spread_pair, -flip_sign * spread_pair], axis=1).reshape(sources)
    moved_rows = 3 * quarter + extra_rows
    others = experts_all - 1
    vary_rows = jax.random.randint(key_list[4], (sources, others), 0, quarter + 1)
    swing_rows = vary_rows - jnp.roll(vary_rows, -1, axis=1)
    source_ids = jnp.arange(sources, dtype=jnp.int32)[:, None]
    other_ids = jnp.arange(others, dtype=jnp.int32)[None, :]
    cyclic = (other_ids - source_ids) % others
    taken_rows = moved_rows[:, None] // others + (cyclic < moved_rows[:, None] % others).astype(jnp.int32)
    other_count = mean_count + swing_rows - taken_rows
    expert_ids = other_ids[0] + (other_ids[0] >= hot_expert).astype(jnp.int32)
    counts = jnp.zeros((sources, experts_all), jnp.int32)
    counts = counts.at[:, expert_ids].set(other_count)
    counts = counts.at[:, hot_expert].set(mean_count + moved_rows)
    bounds = jnp.cumsum(counts, axis=1)
    places = jnp.arange(TOK_DEV * TOPK, dtype=jnp.int32)
    sequence = jnp.sum((bounds[:, None, :] <= places[None, :, None]).astype(jnp.int32), axis=2)
    route_table = sequence.reshape(sources, TOPK, TOK_DEV).transpose(0, 2, 1)

    def shuffle_one(row_key):
        return jax.random.permutation(row_key, TOK_DEV)
    orders = jax.vmap(shuffle_one)(jax.random.split(key_list[5], sources))
    shuffled = jnp.take_along_axis(route_table, orders[:, :, None], axis=1)
    return shuffled.reshape(sources * TOK_DEV, TOPK).astype(jnp.int32)


def levels(rng, extent, cuts, smallest, largest):
    def one(position, blocks):
        draws = jax.random.uniform(jax.random.fold_in(jax.random.fold_in(rng, 6), position), (blocks,), jnp.float32, smallest / len(cuts), largest / len(cuts))
        return jnp.repeat(jnp.exp(draws), extent[position] // blocks).reshape((-1,) + (1,) * (len(extent) - position - 1))

    level = one(*cuts[0])
    for cut in cuts[1:]:
        level = level * one(*cut)
    return level


def normal_values(stream_key, extent, spread, most, cuts=(), held_as=jnp.bfloat16):
    level = levels(stream_key, extent, cuts, -0.22, 0.18) if cuts else 1.0
    result = jax.random.normal(stream_key, extent, jnp.float32) * spread * level
    return jnp.minimum(jnp.maximum(result, -most), most).astype(held_as)


def setup_inputs(seed: int = 0) -> dict:
    splits = jax.random.split(jax.random.key(seed), 8)
    tokens = normal_values(splits[0], (TOKENS, D), 1.0, 6.0, ((0, 64), (1, 8)))
    cotangent = normal_values(splits[1], (TOKENS, D), 1.0, 6.0, ((0, 64), (1, 8)))
    routes = draw_routes(jax.random.fold_in(splits[7], 71), 0)
    mix_weights = jnp.clip(jnp.exp(math.log(0.5) - 2.3025851 * jax.random.uniform(splits[3], (TOKENS, TOPK), jnp.float32) ** levels(splits[3], (TOKENS, TOPK), ((0, 64),), -0.2, 0.2)), 0.05, 0.5)
    w_gate = normal_values(splits[4], (EXPERTS, D, FF), D ** -0.5, 0.125, ((0, 64), (1, 8)))
    w_up = normal_values(splits[5], (EXPERTS, D, FF), D ** -0.5, 0.125, ((0, 64), (1, 8)))
    w_down = normal_values(splits[6], (EXPERTS, FF, D), FF ** -0.5, 0.3125, ((0, 64), (2, 8)))
    return dict(tokens=tokens, cotangent=cotangent, routes=routes, mix_weights=mix_weights, w_gate=w_gate, w_up=w_up, w_down=w_down)


def silu_parts(gate_in):
    logistic = jax.nn.sigmoid(gate_in)
    return gate_in * logistic, logistic * (1.0 + gate_in * (1.0 - logistic))


def block_sum(left_side, right_side):
    partial_sums = jnp.einsum("rpd,pdf->prf", left_side, right_side)
    rounded = lax.optimization_barrier(partial_sums.astype(jnp.bfloat16))
    return jnp.sum(rounded.astype(jnp.float32), axis=0)


def reference(tokens, cotangent, routes, mix_weights, w_gate, w_up, w_down):
    tok_count, model_width = tokens.shape
    picks_per = routes.shape[1]
    expert_count = w_gate.shape[0]
    hidden = w_gate.shape[2]
    flat_routes = routes.reshape(-1).astype(jnp.int32)
    sorted_at = jnp.argsort(flat_routes, stable=True).astype(jnp.int32)
    owner_ids = jnp.arange(expert_count, dtype=jnp.int32)
    counts = jnp.sum((flat_routes[:, None] == owner_ids[None, :]).astype(jnp.int32), axis=0)
    starts = (jnp.cumsum(counts) - counts).astype(jnp.int32)
    padded_order = jnp.concatenate([sorted_at, jnp.zeros((EXP_CAP,), jnp.int32)])
    row_index = jnp.arange(EXP_CAP, dtype=jnp.int32)

    def one_expert(carried, expert):
        mixed_sum, grad_sum = carried
        picked = lax.dynamic_slice(padded_order, (starts[expert],), (EXP_CAP,))
        valid_row = row_index < counts[expert]
        token_at = (picked // picks_per).astype(jnp.int32)
        pick_at = (picked % picks_per).astype(jnp.int32)
        rows_in = jnp.where(valid_row[:, None], tokens[token_at], jnp.zeros((), jnp.bfloat16))
        weight_at = jnp.where(valid_row, mix_weights[token_at, pick_at], jnp.zeros((), jnp.float32))
        out_grad = (weight_at[:, None] * cotangent[token_at].astype(jnp.float32)).astype(jnp.bfloat16)
        gate_matrix = w_gate[expert]
        up_matrix = w_up[expert]
        down_matrix = w_down[expert]
        row_blocks = rows_in.astype(jnp.float32).reshape(EXP_CAP, N_DP, DPART)
        gate_in = block_sum(row_blocks, gate_matrix.astype(jnp.float32).reshape(N_DP, DPART, hidden))
        up_in = block_sum(row_blocks, up_matrix.astype(jnp.float32).reshape(N_DP, DPART, hidden))
        activated, slope_silu = silu_parts(gate_in)
        hidden_act = (activated * up_in).astype(jnp.bfloat16)
        expert_out = jnp.dot(hidden_act, down_matrix, preferred_element_type=jnp.float32).astype(jnp.bfloat16)
        mixed_sum = mixed_sum.at[token_at].add(weight_at[:, None] * expert_out.astype(jnp.float32))
        grad_blocks = out_grad.astype(jnp.float32).reshape(EXP_CAP, N_DP, DPART)
        down_blocks = down_matrix.astype(jnp.float32).reshape(hidden, N_DP, DPART).transpose(1, 2, 0)
        hidden_grad = block_sum(grad_blocks, down_blocks)
        gate_back = (hidden_grad * up_in * slope_silu).astype(jnp.bfloat16)
        up_back = (hidden_grad * activated).astype(jnp.bfloat16)
        row_grad = (jnp.dot(gate_back, gate_matrix.T, preferred_element_type=jnp.float32)
                    + jnp.dot(up_back, up_matrix.T, preferred_element_type=jnp.float32)).astype(jnp.bfloat16)
        grad_sum = grad_sum.at[token_at].add(jnp.where(valid_row[:, None], row_grad.astype(jnp.float32), jnp.zeros((), jnp.float32)))
        gate_grad = jnp.dot(rows_in.T, gate_back, preferred_element_type=jnp.float32)
        up_grad = jnp.dot(rows_in.T, up_back, preferred_element_type=jnp.float32)
        down_grad = jnp.dot(hidden_act.T, out_grad, preferred_element_type=jnp.float32)
        return (mixed_sum, grad_sum), (gate_grad, up_grad, down_grad)

    start_sums = (jnp.zeros((tok_count, model_width), jnp.float32), jnp.zeros((tok_count, model_width), jnp.float32))
    (mixed_sum, grad_sum), (gate_grads, up_grads, down_grads) = lax.scan(one_expert, start_sums, jnp.arange(expert_count, dtype=jnp.int32))
    return (mixed_sum.astype(jnp.bfloat16), grad_sum.astype(jnp.bfloat16), gate_grads, up_grads, down_grads)
```

```python
import jax
import jax.numpy as jnp
from jax import lax
from jax.sharding import PartitionSpec as P


def contract(left_side, right_side, left_dim, right_dim):
    return lax.dot_general(
        left_side,
        right_side,
        (((left_dim,), (right_dim,)), ((), ())),
        preferred_element_type=jnp.float32,
    )


def silu_parts(gate_in):
    logistic = jax.nn.sigmoid(gate_in)
    return (gate_in * logistic, logistic * (1.0 + gate_in * (1.0 - logistic)))


def split_three(values):
    high = values.astype(jnp.bfloat16)
    rest = values - high.astype(jnp.float32)
    middle = rest.astype(jnp.bfloat16)
    low = (rest - middle.astype(jnp.float32)).astype(jnp.bfloat16)
    return (high, middle, low)


def shards(tokens, cotangent, routes, mix_weights, w_gate, w_up, w_down):
    tok_rows, width_dev = tokens.shape
    picks_per = routes.shape[1]
    dp_count = lax.axis_size("dp")
    owner_count = lax.axis_size("expert")
    hidden = w_gate.shape[2]
    sub_rows = tok_rows // dp_count
    width = width_dev * dp_count
    me_dp = lax.axis_index("dp")
    me_expert = lax.axis_index("expert")

    weights_dev = jnp.concatenate([w_gate[0], w_up[0], w_down[0].T], axis=1)
    weights = lax.all_gather(weights_dev, "dp", axis=0, tiled=True)

    both = jnp.stack([tokens, cotangent]).reshape(2, dp_count, sub_rows, width_dev)
    both = lax.all_to_all(both, "dp", split_axis=1, concat_axis=1, tiled=True)
    both = both.transpose(2, 0, 1, 3).reshape(sub_rows, 2 * width)
    my_routes = lax.dynamic_slice_in_dim(routes, me_dp * sub_rows, sub_rows, 0)
    my_mix = lax.dynamic_slice_in_dim(mix_weights, me_dp * sub_rows, sub_rows, 0)
    extra = jnp.concatenate(
        [my_routes.astype(jnp.bfloat16), *split_three(my_mix)], axis=1
    )
    extra = jnp.pad(extra, ((0, 0), (0, 128 - extra.shape[1])))
    rows = lax.all_gather(
        jnp.concatenate([both, extra], axis=1), "expert", axis=0, tiled=True
    )
    x_rows = rows[:, :width]
    c_rows = rows[:, width : 2 * width]
    tail = rows[:, 2 * width : 2 * width + 4 * picks_per].astype(jnp.float32)
    tail = tail.reshape(-1, 4, picks_per)
    mix_all = tail[:, 1] + tail[:, 2] + tail[:, 3]
    named = tail[:, 0] == me_expert.astype(jnp.float32)
    weight_row = jnp.sum(jnp.where(named, mix_all, 0.0), axis=1, keepdims=True)

    w_in = weights[:, : 2 * hidden]
    w_out = weights[:, 2 * hidden :]
    pre = contract(x_rows, w_in, 1, 0)
    back_hidden = contract(c_rows, w_out, 1, 0) * weight_row
    gate_in, up_in = pre[:, :hidden], pre[:, hidden:]
    activated, slope_silu = silu_parts(gate_in)
    hidden_mix = (activated * up_in * weight_row).astype(jnp.bfloat16)
    gate_back = (back_hidden * up_in * slope_silu).astype(jnp.bfloat16)
    up_back = (back_hidden * activated).astype(jnp.bfloat16)
    in_back = jnp.concatenate([gate_back, up_back], axis=1)

    mixed_part = contract(hidden_mix, w_out, 1, 1).astype(jnp.bfloat16)
    grad_part = contract(in_back, w_in, 1, 1).astype(jnp.bfloat16)
    sums = lax.psum_scatter(
        jnp.concatenate([mixed_part, grad_part], axis=1),
        "expert",
        scatter_dimension=0,
        tiled=True,
    )
    in_grad = contract(x_rows, in_back, 0, 0).astype(jnp.bfloat16)
    out_grad = contract(c_rows, hidden_mix, 0, 0).astype(jnp.bfloat16)
    weight_grads = lax.psum_scatter(
        jnp.concatenate([in_grad, out_grad], axis=1), "dp", scatter_dimension=0, tiled=True
    ).astype(jnp.float32)
    sums = sums.reshape(sub_rows, 2, dp_count, width_dev).transpose(1, 2, 0, 3)
    sums = lax.all_to_all(sums, "dp", split_axis=1, concat_axis=1, tiled=True)
    sums = sums.reshape(2, tok_rows, width_dev)
    return (
        sums[0],
        sums[1],
        weight_grads[None, :, :hidden],
        weight_grads[None, :, hidden : 2 * hidden],
        weight_grads[:, 2 * hidden :].T[None],
    )


def solution(mesh):
    placed = (
        P("expert", "dp"),
        P("expert", "dp"),
        P("expert", None),
        P("expert", None),
        P("expert", "dp", None),
        P("expert", "dp", None),
        P("expert", None, "dp"),
    )
    return jax.shard_map(
        shards,
        mesh=mesh,
        in_specs=placed,
        out_specs=(
            P("expert", "dp"),
            P("expert", "dp"),
            P("expert", "dp", None),
            P("expert", "dp", None),
            P("expert", None, "dp"),
        ),
        check_vma=False,
    )
```

```python
import functools

import jax
import jax.numpy as jnp
from jax import lax
from jax.experimental import pallas as pl
from jax.experimental.pallas import tpu as pltpu
from jax.sharding import PartitionSpec as P


def contract(left_side, right_side, left_dim, right_dim):
    return lax.dot_general(
        left_side,
        right_side,
        (((left_dim,), (right_dim,)), ((), ())),
        preferred_element_type=jnp.float32,
    )


def silu_parts(gate_in):
    logistic = jax.nn.sigmoid(gate_in)
    return (gate_in * logistic, logistic * (1.0 + gate_in * (1.0 - logistic)))


def split_three(values):
    high = values.astype(jnp.bfloat16)
    rest = values - high.astype(jnp.float32)
    middle = rest.astype(jnp.bfloat16)
    low = (rest - middle.astype(jnp.float32)).astype(jnp.bfloat16)
    return (high, middle, low)


SIDE_Y = 4
PIECES = 2


def steps_of(count):
    return (count // 2, count - 1 - count // 2)


def ring_places(side_z):
    me = lax.axis_index("expert")
    y_at, z_at = me // side_z, lax.rem(me, side_z)

    def along_z(offset):
        return {"expert": y_at * side_z + lax.rem(z_at + offset + side_z, side_z)}

    def along_y(offset):
        return {"expert": lax.rem(y_at + offset + SIDE_Y, SIDE_Y) * side_z + z_at}

    return (y_at, z_at, along_y, along_z)


def greet(places):
    barrier = pltpu.get_barrier_semaphore()
    for place in places:
        pl.semaphore_signal(
            barrier, inc=1, device_id=place, device_id_type=pl.DeviceIdType.MESH
        )
    pl.semaphore_wait(barrier, len(places))


def send(source, target, sems, place):
    copy = pltpu.make_async_remote_copy(
        src_ref=source,
        dst_ref=target,
        send_sem=sems[0],
        recv_sem=sems[1],
        device_id=place,
        device_id_type=pl.DeviceIdType.MESH,
    )
    copy.start()
    return copy


def gather_kernel(side_z, own_ref, all_ref, y_send, y_recv, z_send, z_recv, own_sem):
    y_at, z_at, along_y, along_z = ring_places(side_z)
    own = pltpu.make_async_copy(own_ref, all_ref.at[y_at, z_at], own_sem)
    own.start()
    greet([along_y(1), along_y(-1), along_z(1), along_z(-1)])

    def wrap(value, count):
        return lax.rem(value + 2 * count, count)

    sent = []
    first = send(own_ref, all_ref.at[y_at, z_at], (y_send.at[0], y_recv.at[0]), along_y(1))
    other = send(own_ref, all_ref.at[y_at, z_at], (y_send.at[1], y_recv.at[1]), along_y(-1))
    first.wait_recv()
    below = wrap(y_at - 1, SIDE_Y)
    second = send(
        all_ref.at[below, z_at], all_ref.at[below, z_at], (y_send.at[2], y_recv.at[2]), along_y(1)
    )
    other.wait_recv()
    second.wait_recv()
    own.wait()
    sent += [first, other, second]
    step_counts = steps_of(side_z)
    span = SIDE_Y // PIECES
    going = {}

    def start(way, step, piece):
        sign = 1 - 2 * way
        block = all_ref.at[pl.ds(piece * span, span), wrap(z_at - sign * step, side_z)]
        at = (way, step, piece)
        going[at] = send(block, block, (z_send.at[at], z_recv.at[at]), along_z(sign))

    for piece in range(PIECES):
        for way in range(2):
            start(way, 0, piece)
    for step in range(step_counts[0]):
        for piece in range(PIECES):
            for way in range(2):
                if step < step_counts[way]:
                    going[(way, step, piece)].wait_recv()
                    if step + 1 < step_counts[way]:
                        start(way, step + 1, piece)
    for copy in sent + list(going.values()):
        copy.wait_send()


def gather_rows(own, side_z):
    rows, columns = own.shape
    longest = steps_of(side_z)[0]
    gathered = pl.pallas_call(
        functools.partial(gather_kernel, side_z),
        out_shape=jax.ShapeDtypeStruct((SIDE_Y, side_z, rows, columns), own.dtype),
        in_specs=[pl.BlockSpec(memory_space=pltpu.VMEM)],
        out_specs=pl.BlockSpec(memory_space=pltpu.VMEM),
        scratch_shapes=[
            pltpu.SemaphoreType.DMA((3,)),
            pltpu.SemaphoreType.DMA((3,)),
            pltpu.SemaphoreType.DMA((2, longest, PIECES)),
            pltpu.SemaphoreType.DMA((2, longest, PIECES)),
            pltpu.SemaphoreType.DMA,
        ],
        compiler_params=pltpu.CompilerParams(
            collective_id=0, has_side_effects=True, vmem_limit_bytes=24 * 2**20
        ),
        cost_estimate=pl.CostEstimate(
            flops=0, bytes_accessed=200 * 2**20, transcendentals=0
        ),
    )(own)
    return gathered.reshape(-1, columns)


def scatter_kernel(side_z, part_ref, sum_ref, got_up, got_down, y_held, y_got,
                   z_send, z_recv, y_send, y_recv):
    y_at, z_at, along_y, along_z = ring_places(side_z)
    greet([along_y(1), along_y(-1), along_z(1), along_z(-1)])

    def wrap(value, count):
        return lax.rem(value + 2 * count, count)

    step_counts = steps_of(side_z)
    span = SIDE_Y // PIECES
    got = (got_up, got_down)
    going = {}

    def target_of(way, step):
        offset = step_counts[way] - step
        return wrap(z_at + (1 - 2 * way) * offset, side_z)

    def start(way, step, piece):
        rows = pl.ds(piece * span, span)
        if step == 0:
            block = part_ref.at[rows, target_of(way, 0)]
        else:
            block = got[way].at[step - 1, rows]
        at = (way, step, piece)
        going[at] = send(
            block,
            got[way].at[step, rows],
            (z_send.at[at], z_recv.at[at]),
            along_z(1 - 2 * way),
        )

    for piece in range(PIECES):
        for way in range(2):
            start(way, 0, piece)
    for step in range(step_counts[0] - 1):
        for piece in range(PIECES):
            for way in range(2):
                if step + 1 < step_counts[way]:
                    going[(way, step, piece)].wait_recv()
                    place = target_of(way, step + 1)

                    def add_own(row, carry, way=way, step=step, place=place):
                        held = got[way][step, row].astype(jnp.float32)
                        mine = part_ref[row, place].astype(jnp.float32)
                        got[way][step, row] = (held + mine).astype(jnp.bfloat16)
                        return carry

                    lax.fori_loop(piece * span, (piece + 1) * span, add_own, 0)
                    start(way, step + 1, piece)
    for way in range(2):
        for piece in range(PIECES):
            going[(way, step_counts[way] - 1, piece)].wait_recv()

    def close(row, carry):
        total = part_ref[row, z_at].astype(jnp.float32)
        total = total + got_up[step_counts[0] - 1, row].astype(jnp.float32)
        total = total + got_down[step_counts[1] - 1, row].astype(jnp.float32)
        y_held[row] = total.astype(jnp.bfloat16)
        return carry

    lax.fori_loop(0, SIDE_Y, close, 0)
    far = send(
        y_held.at[wrap(y_at + 2, SIDE_Y)], y_got.at[0], (y_send.at[0], y_recv.at[0]), along_y(1)
    )
    down = send(
        y_held.at[wrap(y_at - 1, SIDE_Y)], y_got.at[1], (y_send.at[1], y_recv.at[1]), along_y(-1)
    )
    far.wait_recv()
    up_row = y_held[wrap(y_at + 1, SIDE_Y)].astype(jnp.float32)
    y_got[0] = (y_got[0].astype(jnp.float32) + up_row).astype(jnp.bfloat16)
    near = send(y_got.at[0], y_got.at[2], (y_send.at[2], y_recv.at[2]), along_y(1))
    down.wait_recv()
    near.wait_recv()
    total = y_held[y_at].astype(jnp.float32) + y_got[1].astype(jnp.float32)
    sum_ref[...] = (total + y_got[2].astype(jnp.float32)).astype(jnp.bfloat16)
    for copy in [far, down, near] + list(going.values()):
        copy.wait_send()


def scatter_sums(parts, side_z):
    all_rows, columns = parts.shape
    rows = all_rows // (SIDE_Y * side_z)
    up_steps, down_steps = steps_of(side_z)
    return pl.pallas_call(
        functools.partial(scatter_kernel, side_z),
        out_shape=jax.ShapeDtypeStruct((rows, columns), parts.dtype),
        in_specs=[pl.BlockSpec(memory_space=pltpu.VMEM)],
        out_specs=pl.BlockSpec(memory_space=pltpu.VMEM),
        scratch_shapes=[
            pltpu.VMEM((up_steps, SIDE_Y, rows, columns), parts.dtype),
            pltpu.VMEM((down_steps, SIDE_Y, rows, columns), parts.dtype),
            pltpu.VMEM((SIDE_Y, rows, columns), parts.dtype),
            pltpu.VMEM((3, rows, columns), parts.dtype),
            pltpu.SemaphoreType.DMA((2, up_steps, PIECES)),
            pltpu.SemaphoreType.DMA((2, up_steps, PIECES)),
            pltpu.SemaphoreType.DMA((3,)),
            pltpu.SemaphoreType.DMA((3,)),
        ],
        compiler_params=pltpu.CompilerParams(
            collective_id=1, has_side_effects=True, vmem_limit_bytes=32 * 2**20
        ),
        cost_estimate=pl.CostEstimate(
            flops=0, bytes_accessed=200 * 2**20, transcendentals=0
        ),
    )(parts.reshape(SIDE_Y, side_z, rows, columns))


def shards(tokens, cotangent, routes, mix_weights, w_gate, w_up, w_down):
    tok_rows, width_dev = tokens.shape
    picks_per = routes.shape[1]
    dp_count = lax.axis_size("dp")
    owner_count = lax.axis_size("expert")
    hidden = w_gate.shape[2]
    sub_rows = tok_rows // dp_count
    width = width_dev * dp_count
    me_dp = lax.axis_index("dp")
    me_expert = lax.axis_index("expert")

    weights_dev = jnp.concatenate([w_gate[0], w_up[0], w_down[0].T], axis=1)
    weights = lax.all_gather(weights_dev, "dp", axis=0, tiled=True)

    both = jnp.stack([tokens, cotangent]).reshape(2, dp_count, sub_rows, width_dev)
    both = lax.all_to_all(both, "dp", split_axis=1, concat_axis=1, tiled=True)
    both = both.transpose(2, 0, 1, 3).reshape(sub_rows, 2 * width)
    my_routes = lax.dynamic_slice_in_dim(routes, me_dp * sub_rows, sub_rows, 0)
    my_mix = lax.dynamic_slice_in_dim(mix_weights, me_dp * sub_rows, sub_rows, 0)
    extra = jnp.concatenate(
        [my_routes.astype(jnp.bfloat16), *split_three(my_mix)], axis=1
    )
    extra = jnp.pad(extra, ((0, 0), (0, 128 - extra.shape[1])))
    rows = gather_rows(jnp.concatenate([both, extra], axis=1), owner_count // SIDE_Y)
    x_rows = rows[:, :width]
    c_rows = rows[:, width : 2 * width]
    tail = rows[:, 2 * width : 2 * width + 4 * picks_per].astype(jnp.float32)
    tail = tail.reshape(-1, 4, picks_per)
    mix_all = tail[:, 1] + tail[:, 2] + tail[:, 3]
    named = tail[:, 0] == me_expert.astype(jnp.float32)
    weight_row = jnp.sum(jnp.where(named, mix_all, 0.0), axis=1, keepdims=True)

    w_in = weights[:, : 2 * hidden]
    w_out = weights[:, 2 * hidden :]
    pre = contract(x_rows, w_in, 1, 0)
    back_hidden = contract(c_rows, w_out, 1, 0) * weight_row
    gate_in, up_in = pre[:, :hidden], pre[:, hidden:]
    activated, slope_silu = silu_parts(gate_in)
    hidden_mix = (activated * up_in * weight_row).astype(jnp.bfloat16)
    gate_back = (back_hidden * up_in * slope_silu).astype(jnp.bfloat16)
    up_back = (back_hidden * activated).astype(jnp.bfloat16)
    in_back = jnp.concatenate([gate_back, up_back], axis=1)

    mixed_part = contract(hidden_mix, w_out, 1, 1).astype(jnp.bfloat16)
    grad_part = contract(in_back, w_in, 1, 1).astype(jnp.bfloat16)
    in_grad = contract(x_rows, in_back, 0, 0).astype(jnp.bfloat16)
    out_grad = contract(c_rows, hidden_mix, 0, 0).astype(jnp.bfloat16)
    weight_grads = lax.psum_scatter(
        jnp.concatenate([in_grad, out_grad], axis=1), "dp", scatter_dimension=0, tiled=True
    ).astype(jnp.float32)
    sums = scatter_sums(
        jnp.concatenate([mixed_part, grad_part], axis=1), owner_count // SIDE_Y
    )
    sums = sums.reshape(sub_rows, 2, dp_count, width_dev).transpose(1, 2, 0, 3)
    sums = lax.all_to_all(sums, "dp", split_axis=1, concat_axis=1, tiled=True)
    sums = sums.reshape(2, tok_rows, width_dev)
    return (
        sums[0],
        sums[1],
        weight_grads[None, :, :hidden],
        weight_grads[None, :, hidden : 2 * hidden],
        weight_grads[:, 2 * hidden :].T[None],
    )


def solution(mesh):
    placed = (
        P("expert", "dp"),
        P("expert", "dp"),
        P("expert", None),
        P("expert", None),
        P("expert", "dp", None),
        P("expert", "dp", None),
        P("expert", None, "dp"),
    )
    return jax.shard_map(
        shards,
        mesh=mesh,
        in_specs=placed,
        out_specs=(
            P("expert", "dp"),
            P("expert", "dp"),
            P("expert", "dp", None),
            P("expert", "dp", None),
            P("expert", None, "dp"),
        ),
        check_vma=False,
    )
```

```python
import functools

import jax
import jax.numpy as jnp
from jax import lax
from jax.experimental import pallas as pl
from jax.experimental.pallas import tpu as pltpu
from jax.sharding import PartitionSpec as P


def contract(left_side, right_side, left_dim, right_dim):
    return lax.dot_general(
        left_side,
        right_side,
        (((left_dim,), (right_dim,)), ((), ())),
        preferred_element_type=jnp.float32,
    )


def silu_parts(gate_in):
    logistic = jax.nn.sigmoid(gate_in)
    return (gate_in * logistic, logistic * (1.0 + gate_in * (1.0 - logistic)))


def split_three(values):
    high = values.astype(jnp.bfloat16)
    rest = values - high.astype(jnp.float32)
    middle = rest.astype(jnp.bfloat16)
    low = (rest - middle.astype(jnp.float32)).astype(jnp.bfloat16)
    return (high, middle, low)


SIDE_Y = 4
PIECES = 2


def steps_of(count):
    return (count // 2, count - 1 - count // 2)


def ring_places(side_z):
    me = lax.axis_index("expert")
    y_at, z_at = me // side_z, lax.rem(me, side_z)

    def along_z(offset):
        return {"expert": y_at * side_z + lax.rem(z_at + offset + side_z, side_z)}

    def along_y(offset):
        return {"expert": lax.rem(y_at + offset + SIDE_Y, SIDE_Y) * side_z + z_at}

    return (y_at, z_at, along_y, along_z)


def greet(places):
    barrier = pltpu.get_barrier_semaphore()
    for place in places:
        pl.semaphore_signal(
            barrier, inc=1, device_id=place, device_id_type=pl.DeviceIdType.MESH
        )
    pl.semaphore_wait(barrier, len(places))


def send(source, target, sems, place):
    copy = pltpu.make_async_remote_copy(
        src_ref=source,
        dst_ref=target,
        send_sem=sems[0],
        recv_sem=sems[1],
        device_id=place,
        device_id_type=pl.DeviceIdType.MESH,
    )
    copy.start()
    return copy


def wrap(value, count):
    return lax.rem(value + 2 * count, count)


def gather_kernel(side_z, x_own, c_own, x_all, c_all, xz_send, xz_recv, xy_send, xy_recv,
                  cy_send, cy_recv, cz_send, cz_recv, own_sem):
    y_at, z_at, along_y, along_z = ring_places(side_z)
    own_copies = [
        pltpu.make_async_copy(x_own, x_all.at[y_at, z_at], own_sem.at[0]),
        pltpu.make_async_copy(c_own, c_all.at[y_at, z_at], own_sem.at[1]),
    ]
    for copy in own_copies:
        copy.start()
    greet([along_y(1), along_y(-1), along_z(1), along_z(-1)])
    for copy in own_copies:
        copy.wait()
    step_counts = steps_of(side_z)
    span = SIDE_Y // PIECES
    up_y, down_y = wrap(y_at - 1, SIDE_Y), wrap(y_at + 1, SIDE_Y)
    xz, xy, cz = {}, {}, {}

    def start_xz(way, step):
        sign = 1 - 2 * way
        block = x_all.at[y_at, wrap(z_at - sign * step, side_z)]
        at = (way, step)
        xz[at] = send(block, block, (xz_send.at[at], xz_recv.at[at]), along_z(sign))

    def place_of(number):
        sign = 1 if number % 2 else -1
        return wrap(z_at - sign * ((number + 1) // 2), side_z)

    def start_xy(number, hop):
        row = up_y if hop == 2 else y_at
        block = x_all.at[row, place_of(number)]
        at = (number, hop)
        xy[at] = send(
            block, block, (xy_send.at[at], xy_recv.at[at]), along_y(-1 if hop == 1 else 1)
        )

    def start_cz(way, step, piece):
        sign = 1 - 2 * way
        block = c_all.at[pl.ds(piece * span, span), wrap(z_at - sign * step, side_z)]
        at = (way, step, piece)
        cz[at] = send(block, block, (cz_send.at[at], cz_recv.at[at]), along_z(sign))

    start_xz(0, 0)
    start_xz(1, 0)
    mine = c_all.at[y_at, z_at]
    first = send(mine, mine, (cy_send.at[0], cy_recv.at[0]), along_y(1))
    other = send(mine, mine, (cy_send.at[1], cy_recv.at[1]), along_y(-1))
    start_xy(0, 0)
    start_xy(0, 1)
    first.wait_recv()
    below = c_all.at[up_y, z_at]
    second = send(below, below, (cy_send.at[2], cy_recv.at[2]), along_y(1))
    other.wait_recv()
    second.wait_recv()
    for piece in range(PIECES):
        for way in range(2):
            start_cz(way, 0, piece)
    passed = 0
    arrived = 1
    for step in range(step_counts[0]):
        ready = arrived
        for way in range(2):
            if step < step_counts[way]:
                xz[(way, step)].wait_recv()
                if step + 1 < step_counts[way]:
                    start_xz(way, step + 1)
                start_xy(2 * step + 1 + way, 0)
                start_xy(2 * step + 1 + way, 1)
                arrived += 1
        for number in range(passed, ready):
            xy[(number, 0)].wait_recv()
            start_xy(number, 2)
        passed = ready
        for piece in range(PIECES):
            for way in range(2):
                if step < step_counts[way]:
                    cz[(way, step, piece)].wait_recv()
                    if step + 1 < step_counts[way]:
                        start_cz(way, step + 1, piece)
    for number in range(passed, side_z):
        xy[(number, 0)].wait_recv()
        start_xy(number, 2)
    for number in range(side_z):
        xy[(number, 1)].wait_recv()
        xy[(number, 2)].wait_recv()
    for group in (xz, xy, cz):
        for copy in group.values():
            copy.wait_send()
    for copy in (first, other, second):
        copy.wait_send()


def gather_rows(x_own, c_own, side_z):
    rows = x_own.shape[0]
    longest = steps_of(side_z)[0]
    vmem = pl.BlockSpec(memory_space=pltpu.VMEM)
    sem = pltpu.SemaphoreType.DMA
    gathered = pl.pallas_call(
        functools.partial(gather_kernel, side_z),
        out_shape=[
            jax.ShapeDtypeStruct((SIDE_Y, side_z, *own.shape), own.dtype)
            for own in (x_own, c_own)
        ],
        in_specs=[vmem, vmem],
        out_specs=[vmem, vmem],
        scratch_shapes=[
            sem((2, longest)),
            sem((2, longest)),
            sem((side_z, 3)),
            sem((side_z, 3)),
            sem((3,)),
            sem((3,)),
            sem((2, longest, PIECES)),
            sem((2, longest, PIECES)),
            sem((2,)),
        ],
        compiler_params=pltpu.CompilerParams(
            collective_id=0, has_side_effects=True, vmem_limit_bytes=24 * 2**20
        ),
        cost_estimate=pl.CostEstimate(
            flops=0, bytes_accessed=200 * 2**20, transcendentals=0
        ),
    )(x_own, c_own)
    return [whole.reshape(SIDE_Y * side_z * rows, -1) for whole in gathered]


def scatter_kernel(side_z, m_part, g_part, m_sum, g_sum, m_up, m_down, m_held, m_got,
                   g_y, g_held, g_up, g_down, mz_send, mz_recv, my_send, my_recv,
                   gy_send, gy_recv, gz_send, gz_recv):
    y_at, z_at, along_y, along_z = ring_places(side_z)
    greet([along_y(1), along_y(-1), along_z(1), along_z(-1)])
    step_counts = steps_of(side_z)
    span = SIDE_Y // PIECES
    half = side_z // 2
    m_slots, g_slots = (m_up, m_down), (g_up, g_down)
    mz, gz, gy = {}, {}, {}

    def rounded_sum(*terms):
        total = terms[0].astype(jnp.float32)
        for term in terms[1:]:
            total = total + term.astype(jnp.float32)
        return total.astype(jnp.bfloat16)

    def target_of(way, step):
        return wrap(z_at + (1 - 2 * way) * (step_counts[way] - step), side_z)

    def start_mz(way, step, piece):
        rows = pl.ds(piece * span, span)
        block = m_part.at[rows, target_of(way, 0)] if step == 0 else m_slots[way].at[step - 1, rows]
        at = (way, step, piece)
        mz[at] = send(
            block, m_slots[way].at[step, rows], (mz_send.at[at], mz_recv.at[at]), along_z(1 - 2 * way)
        )

    def start_gz(way, step):
        block = g_held.at[target_of(way, 0)] if step == 0 else g_slots[way].at[step - 1]
        at = (way, step)
        gz[at] = send(
            block, g_slots[way].at[step], (gz_send.at[at], gz_recv.at[at]), along_z(1 - 2 * way)
        )

    def start_gy(slot, source, way):
        gy[slot] = send(
            source, g_y.at[slot], (gy_send.at[slot], gy_recv.at[slot]), along_y(1 - 2 * way)
        )

    low, high = pl.ds(0, half), pl.ds(half, half)
    above, below, across = wrap(y_at + 1, SIDE_Y), wrap(y_at - 1, SIDE_Y), wrap(y_at + 2, SIDE_Y)

    def pass_far():
        for slot, row, first, way in ((0, above, 0, 0), (1, below, half, 1)):
            gy[slot].wait_recv()

            def add_row(place, carry, slot=slot, row=row, first=first):
                g_y[slot, place] = rounded_sum(g_y[slot, place], g_part[row, first + place])
                return carry

            lax.fori_loop(0, half, add_row, 0)
            start_gy(4 + slot, g_y.at[slot], way)

    def close_y():
        for slot in (2, 3, 4, 5):
            gy[slot].wait_recv()

        def add_low(place, carry):
            g_held[place] = rounded_sum(g_part[y_at, place], g_y[4, place], g_y[3, place])
            return carry

        def add_high(place, carry):
            g_held[half + place] = rounded_sum(
                g_part[y_at, half + place], g_y[2, place], g_y[5, place]
            )
            return carry

        lax.fori_loop(0, half, add_low, 0)
        lax.fori_loop(0, half, add_high, 0)
        start_gz(0, 0)
        start_gz(1, 0)

    def step_gz(step):
        for way in range(2):
            if step + 1 < step_counts[way]:
                gz[(way, step)].wait_recv()
                slot = g_slots[way]
                slot[step] = rounded_sum(slot[step], g_held[target_of(way, step + 1)])
                start_gz(way, step + 1)

    for piece in range(PIECES):
        for way in range(2):
            start_mz(way, 0, piece)
    start_gy(0, g_part.at[across, low], 0)
    start_gy(1, g_part.at[across, high], 1)
    start_gy(2, g_part.at[above, high], 0)
    start_gy(3, g_part.at[below, low], 1)
    middle = step_counts[0] // 2
    g_step = 0
    for step in range(step_counts[0] - 1):
        for piece in range(PIECES):
            for way in range(2):
                if step + 1 < step_counts[way]:
                    mz[(way, step, piece)].wait_recv()
                    place = target_of(way, step + 1)

                    def add_own(row, carry, way=way, step=step, place=place):
                        slot = m_slots[way]
                        slot[step, row] = rounded_sum(slot[step, row], m_part[row, place])
                        return carry

                    lax.fori_loop(piece * span, (piece + 1) * span, add_own, 0)
                    start_mz(way, step + 1, piece)
            if step > middle:
                step_gz(g_step)
                g_step += 1
        if step == 1:
            pass_far()
        if step == middle:
            close_y()
    for way in range(2):
        for piece in range(PIECES):
            mz[(way, step_counts[way] - 1, piece)].wait_recv()

    def close_z(row, carry):
        m_held[row] = rounded_sum(
            m_part[row, z_at], m_up[step_counts[0] - 1, row], m_down[step_counts[1] - 1, row]
        )
        return carry

    lax.fori_loop(0, SIDE_Y, close_z, 0)
    far = send(m_held.at[across], m_got.at[0], (my_send.at[0], my_recv.at[0]), along_y(1))
    down = send(m_held.at[below], m_got.at[1], (my_send.at[1], my_recv.at[1]), along_y(-1))
    if g_step < step_counts[0] - 1:
        step_gz(g_step)
        g_step += 1
    far.wait_recv()
    m_got[0] = rounded_sum(m_got[0], m_held[above])
    near = send(m_got.at[0], m_got.at[2], (my_send.at[2], my_recv.at[2]), along_y(1))
    while g_step < step_counts[0] - 1:
        step_gz(g_step)
        g_step += 1
    down.wait_recv()
    near.wait_recv()
    m_sum[...] = rounded_sum(m_held[y_at], m_got[1], m_got[2])
    for way in range(2):
        gz[(way, step_counts[way] - 1)].wait_recv()
    g_sum[...] = rounded_sum(
        g_held[z_at], g_up[step_counts[0] - 1], g_down[step_counts[1] - 1]
    )
    for group in (mz, gz, gy):
        for copy in group.values():
            copy.wait_send()
    for copy in (far, down, near):
        copy.wait_send()


def scatter_sums(m_part, g_part, side_z):
    all_rows, columns = m_part.shape
    rows = all_rows // (SIDE_Y * side_z)
    up_steps, down_steps = steps_of(side_z)
    kind = m_part.dtype
    vmem = pl.BlockSpec(memory_space=pltpu.VMEM)
    sem = pltpu.SemaphoreType.DMA
    whole = (SIDE_Y, side_z, rows, columns)
    return pl.pallas_call(
        functools.partial(scatter_kernel, side_z),
        out_shape=[jax.ShapeDtypeStruct((rows, columns), kind)] * 2,
        in_specs=[vmem, vmem],
        out_specs=[vmem, vmem],
        scratch_shapes=[
            pltpu.VMEM((up_steps, SIDE_Y, rows, columns), kind),
            pltpu.VMEM((down_steps, SIDE_Y, rows, columns), kind),
            pltpu.VMEM((SIDE_Y, rows, columns), kind),
            pltpu.VMEM((3, rows, columns), kind),
            pltpu.VMEM((6, side_z // 2, rows, columns), kind),
            pltpu.VMEM((side_z, rows, columns), kind),
            pltpu.VMEM((up_steps, rows, columns), kind),
            pltpu.VMEM((down_steps, rows, columns), kind),
            sem((2, up_steps, PIECES)),
            sem((2, up_steps, PIECES)),
            sem((3,)),
            sem((3,)),
            sem((6,)),
            sem((6,)),
            sem((2, up_steps)),
            sem((2, up_steps)),
        ],
        compiler_params=pltpu.CompilerParams(
            collective_id=1, has_side_effects=True, vmem_limit_bytes=32 * 2**20
        ),
        cost_estimate=pl.CostEstimate(
            flops=0, bytes_accessed=200 * 2**20, transcendentals=0
        ),
    )(m_part.reshape(whole), g_part.reshape(whole))


def shards(tokens, cotangent, routes, mix_weights, w_gate, w_up, w_down):
    tok_rows, width_dev = tokens.shape
    picks_per = routes.shape[1]
    dp_count = lax.axis_size("dp")
    owner_count = lax.axis_size("expert")
    hidden = w_gate.shape[2]
    sub_rows = tok_rows // dp_count
    width = width_dev * dp_count
    me_dp = lax.axis_index("dp")
    me_expert = lax.axis_index("expert")

    weights_dev = jnp.concatenate([w_gate[0], w_up[0], w_down[0].T], axis=1)
    weights = lax.all_gather(weights_dev, "dp", axis=0, tiled=True)

    both = jnp.stack([tokens, cotangent]).reshape(2, dp_count, sub_rows, width_dev)
    both = lax.all_to_all(both, "dp", split_axis=1, concat_axis=1, tiled=True)
    both = both.transpose(0, 2, 1, 3).reshape(2, sub_rows, width)
    my_routes = lax.dynamic_slice_in_dim(routes, me_dp * sub_rows, sub_rows, 0)
    my_mix = lax.dynamic_slice_in_dim(mix_weights, me_dp * sub_rows, sub_rows, 0)
    extra = jnp.concatenate(
        [my_routes.astype(jnp.bfloat16), *split_three(my_mix)], axis=1
    )
    extra = jnp.pad(extra, ((0, 0), (0, 128 - extra.shape[1])))
    x_rows, c_wide = gather_rows(
        both[0], jnp.concatenate([both[1], extra], axis=1), owner_count // SIDE_Y
    )
    c_rows = c_wide[:, :width]
    tail = c_wide[:, width : width + 4 * picks_per].astype(jnp.float32)
    tail = tail.reshape(-1, 4, picks_per)
    mix_all = tail[:, 1] + tail[:, 2] + tail[:, 3]
    named = tail[:, 0] == me_expert.astype(jnp.float32)
    weight_row = jnp.sum(jnp.where(named, mix_all, 0.0), axis=1, keepdims=True)

    w_in = weights[:, : 2 * hidden]
    w_out = weights[:, 2 * hidden :]
    pre = contract(x_rows, w_in, 1, 0)
    back_hidden = contract(c_rows, w_out, 1, 0) * weight_row
    gate_in, up_in = pre[:, :hidden], pre[:, hidden:]
    activated, slope_silu = silu_parts(gate_in)
    hidden_mix = (activated * up_in * weight_row).astype(jnp.bfloat16)
    gate_back = (back_hidden * up_in * slope_silu).astype(jnp.bfloat16)
    up_back = (back_hidden * activated).astype(jnp.bfloat16)
    in_back = jnp.concatenate([gate_back, up_back], axis=1)

    mixed_part = contract(hidden_mix, w_out, 1, 1).astype(jnp.bfloat16)
    grad_part = contract(in_back, w_in, 1, 1).astype(jnp.bfloat16)
    in_grad = contract(x_rows, in_back, 0, 0).astype(jnp.bfloat16)
    out_grad = contract(c_rows, hidden_mix, 0, 0).astype(jnp.bfloat16)
    weight_grads = lax.psum_scatter(
        jnp.concatenate([in_grad, out_grad], axis=1), "dp", scatter_dimension=0, tiled=True
    ).astype(jnp.float32)
    sums = jnp.stack(scatter_sums(mixed_part, grad_part, owner_count // SIDE_Y))
    sums = sums.reshape(2, sub_rows, dp_count, width_dev).transpose(0, 2, 1, 3)
    sums = lax.all_to_all(sums, "dp", split_axis=1, concat_axis=1, tiled=True)
    sums = sums.reshape(2, tok_rows, width_dev)
    return (
        sums[0],
        sums[1],
        weight_grads[None, :, :hidden],
        weight_grads[None, :, hidden : 2 * hidden],
        weight_grads[:, 2 * hidden :].T[None],
    )


def solution(mesh):
    placed = (
        P("expert", "dp"),
        P("expert", "dp"),
        P("expert", None),
        P("expert", None),
        P("expert", "dp", None),
        P("expert", "dp", None),
        P("expert", None, "dp"),
    )
    return jax.shard_map(
        shards,
        mesh=mesh,
        in_specs=placed,
        out_specs=(
            P("expert", "dp"),
            P("expert", "dp"),
            P("expert", "dp", None),
            P("expert", "dp", None),
            P("expert", None, "dp"),
        ),
        check_vma=False,
    )
```

```python
import functools

import jax
import jax.numpy as jnp
from jax import lax
from jax.experimental import pallas as pl
from jax.experimental.pallas import tpu as pltpu
from jax.sharding import PartitionSpec as P


def contract(left_side, right_side, left_dim, right_dim):
    return lax.dot_general(
        left_side,
        right_side,
        (((left_dim,), (right_dim,)), ((), ())),
        preferred_element_type=jnp.float32,
    )


def silu_parts(gate_in):
    logistic = jax.nn.sigmoid(gate_in)
    return (gate_in * logistic, logistic * (1.0 + gate_in * (1.0 - logistic)))


def split_three(values):
    high = values.astype(jnp.bfloat16)
    rest = values - high.astype(jnp.float32)
    middle = rest.astype(jnp.bfloat16)
    low = (rest - middle.astype(jnp.float32)).astype(jnp.bfloat16)
    return (high, middle, low)


SIDE_Y = 4
PIECES = 2


def steps_of(count):
    return (count // 2, count - 1 - count // 2)


def ring_places(side_z):
    me = lax.axis_index("expert")
    y_at, z_at = me // side_z, lax.rem(me, side_z)

    def along_z(offset):
        return {"expert": y_at * side_z + lax.rem(z_at + offset + side_z, side_z)}

    def along_y(offset):
        return {"expert": lax.rem(y_at + offset + SIDE_Y, SIDE_Y) * side_z + z_at}

    return (y_at, z_at, along_y, along_z)


def greet(places):
    barrier = pltpu.get_barrier_semaphore()
    for place in places:
        pl.semaphore_signal(
            barrier, inc=1, device_id=place, device_id_type=pl.DeviceIdType.MESH
        )
    pl.semaphore_wait(barrier, len(places))


def send(source, target, sems, place):
    copy = pltpu.make_async_remote_copy(
        src_ref=source,
        dst_ref=target,
        send_sem=sems[0],
        recv_sem=sems[1],
        device_id=place,
        device_id_type=pl.DeviceIdType.MESH,
    )
    copy.start()
    return copy


def wrap(value, count):
    return lax.rem(value + 2 * count, count)


def dp_places(dp_count):
    me = lax.axis_index("dp")
    others = [lax.rem(me + hop, dp_count) for hop in range(1, dp_count)]
    return (me, others, [{"dp": other} for other in others])


def part_of(index, size):
    return pl.ds(pl.multiple_of(index * size, size), size)


def gather_kernel(side_z, dp_count, tok_ref, cot_ref, extra_ref, x_all, c_all, xz_send,
                  xz_recv, xy_send, xy_recv, cy_send, cy_recv, cz_send, cz_recv,
                  dp_send, dp_recv, own_sem):
    y_at, z_at, along_y, along_z = ring_places(side_z)
    me, others, other_places = dp_places(dp_count)
    width_dev = tok_ref.shape[1]
    rows = tok_ref.shape[0] // dp_count
    mine = part_of(me, rows)
    columns = part_of(me, width_dev)
    width = pl.ds(dp_count * width_dev, extra_ref.shape[1])
    pairs = ((tok_ref, x_all), (cot_ref, c_all))
    own_copies = [
        pltpu.make_async_copy(held.at[mine], whole.at[y_at, z_at, :, columns], own_sem.at[i])
        for i, (held, whole) in enumerate(pairs)
    ]
    own_copies.append(
        pltpu.make_async_copy(extra_ref, c_all.at[y_at, z_at, :, width], own_sem.at[2])
    )
    for copy in own_copies:
        copy.start()
    greet([along_y(1), along_y(-1), along_z(1), along_z(-1)] + other_places)
    swapped = []
    for i, (held, whole) in enumerate(pairs):
        for hop, (other, place) in enumerate(zip(others, other_places)):
            swapped.append(send(
                held.at[part_of(other, rows)],
                whole.at[y_at, z_at, :, columns],
                (dp_send.at[i, hop], dp_recv.at[i, hop]),
                place,
            ))
    for copy in own_copies:
        copy.wait()
    for copy in swapped:
        copy.wait_recv()
    step_counts = steps_of(side_z)
    up_y, down_y = wrap(y_at - 1, SIDE_Y), wrap(y_at + 1, SIDE_Y)
    held_rows = (y_at, up_y, down_y, wrap(y_at + 2, SIDE_Y))
    xz, xy, cz = {}, {}, {}

    def start_xz(way, step):
        sign = 1 - 2 * way
        block = x_all.at[y_at, wrap(z_at - sign * step, side_z)]
        at = (way, step)
        xz[at] = send(block, block, (xz_send.at[at], xz_recv.at[at]), along_z(sign))

    def place_of(number):
        sign = 1 if number % 2 else -1
        return wrap(z_at - sign * ((number + 1) // 2), side_z)

    def start_xy(number, hop):
        down = number % 2 if hop == 2 else hop
        row = (up_y, down_y)[down] if hop == 2 else y_at
        block = x_all.at[row, place_of(number)]
        at = (number, hop)
        xy[at] = send(
            block, block, (xy_send.at[at], xy_recv.at[at]), along_y(1 - 2 * down)
        )

    def start_cz(way, step, piece):
        sign = 1 - 2 * way
        block = c_all.at[held_rows[piece], wrap(z_at - sign * step, side_z)]
        at = (way, step, piece)
        cz[at] = send(block, block, (cz_send.at[at], cz_recv.at[at]), along_z(sign))

    start_xz(0, 0)
    start_xz(1, 0)
    block = c_all.at[y_at, z_at]
    first = send(block, block, (cy_send.at[0], cy_recv.at[0]), along_y(1))
    other = send(block, block, (cy_send.at[1], cy_recv.at[1]), along_y(-1))
    for way in range(2):
        start_cz(way, 0, 0)
    start_xy(0, 0)
    start_xy(0, 1)
    first.wait_recv()
    below = c_all.at[up_y, z_at]
    second = send(below, below, (cy_send.at[2], cy_recv.at[2]), along_y(1))
    for piece, copy in ((1, None), (2, other), (3, second)):
        if copy is not None:
            copy.wait_recv()
        for way in range(2):
            start_cz(way, 0, piece)
    passed = 0
    arrived = 1
    for step in range(step_counts[0]):
        ready = arrived
        for way in range(2):
            if step < step_counts[way]:
                xz[(way, step)].wait_recv()
                if step + 1 < step_counts[way]:
                    start_xz(way, step + 1)
                start_xy(2 * step + 1 + way, 0)
                start_xy(2 * step + 1 + way, 1)
                arrived += 1
        for number in range(passed, ready):
            xy[(number, number % 2)].wait_recv()
            start_xy(number, 2)
        passed = ready
        for piece in range(SIDE_Y):
            for way in range(2):
                if step < step_counts[way]:
                    cz[(way, step, piece)].wait_recv()
                    if step + 1 < step_counts[way]:
                        start_cz(way, step + 1, piece)
    for number in range(passed, side_z):
        xy[(number, number % 2)].wait_recv()
        start_xy(number, 2)
    for number in range(side_z):
        xy[(number, 1 - number % 2)].wait_recv()
        xy[(number, 2)].wait_recv()
    for group in (xz, xy, cz):
        for copy in group.values():
            copy.wait_send()
    for copy in (first, other, second, *swapped):
        copy.wait_send()


def gather_rows(tokens, cotangent, extra, side_z, dp_count):
    rows = extra.shape[0]
    width = tokens.shape[1] * dp_count
    longest = steps_of(side_z)[0]
    vmem = pl.BlockSpec(memory_space=pltpu.VMEM)
    sem = pltpu.SemaphoreType.DMA
    gathered = pl.pallas_call(
        functools.partial(gather_kernel, side_z, dp_count),
        out_shape=[
            jax.ShapeDtypeStruct((SIDE_Y, side_z, rows, columns), tokens.dtype)
            for columns in (width, width + extra.shape[1])
        ],
        in_specs=[vmem, vmem, vmem],
        out_specs=[vmem, vmem],
        scratch_shapes=[
            sem((2, longest)),
            sem((2, longest)),
            sem((side_z, 3)),
            sem((side_z, 3)),
            sem((3,)),
            sem((3,)),
            sem((2, longest, SIDE_Y)),
            sem((2, longest, SIDE_Y)),
            sem((2, dp_count - 1)),
            sem((2, dp_count - 1)),
            sem((3,)),
        ],
        compiler_params=pltpu.CompilerParams(
            collective_id=0, has_side_effects=True, vmem_limit_bytes=14 * 2**20
        ),
        cost_estimate=pl.CostEstimate(
            flops=0, bytes_accessed=200 * 2**20, transcendentals=0
        ),
    )(tokens, cotangent, extra)
    return [whole.reshape(SIDE_Y * side_z * rows, -1) for whole in gathered]


def scatter_kernel(side_z, dp_count, m_part, g_part, m_out, g_out, m_sum, g_sum, m_up, m_down, m_held, m_got,
                   g_y, g_held, g_up, g_down, mz_send, mz_recv, my_send, my_recv,
                   gy_send, gy_recv, gz_send, gz_recv, dp_send, dp_recv, own_sem):
    y_at, z_at, along_y, along_z = ring_places(side_z)
    me, others, other_places = dp_places(dp_count)
    greet([along_y(1), along_y(-1), along_z(1), along_z(-1)] + other_places)
    width_dev = m_out.shape[1]
    mine = part_of(me, m_out.shape[0] // dp_count)
    columns = part_of(me, width_dev)
    own_copies, swapped = [], []

    def hand_out(i, total, result):
        own_copies.append(
            pltpu.make_async_copy(total.at[:, columns], result.at[mine], own_sem.at[i])
        )
        own_copies[-1].start()
        for hop, (other, place) in enumerate(zip(others, other_places)):
            swapped.append(send(
                total.at[:, part_of(other, width_dev)],
                result.at[mine],
                (dp_send.at[i, hop], dp_recv.at[i, hop]),
                place,
            ))

    step_counts = steps_of(side_z)
    span = SIDE_Y // PIECES
    half = side_z // 2
    m_slots, g_slots = (m_up, m_down), (g_up, g_down)
    mz, gz, gy = {}, {}, {}

    def rounded_sum(*terms):
        total = terms[0].astype(jnp.float32)
        for term in terms[1:]:
            total = total + term.astype(jnp.float32)
        return total.astype(jnp.bfloat16)

    def target_of(way, step):
        return wrap(z_at + (1 - 2 * way) * (step_counts[way] - step), side_z)

    def start_mz(way, step, piece):
        rows = pl.ds(piece * span, span)
        block = m_part.at[rows, target_of(way, 0)] if step == 0 else m_slots[way].at[step - 1, rows]
        at = (way, step, piece)
        mz[at] = send(
            block, m_slots[way].at[step, rows], (mz_send.at[at], mz_recv.at[at]), along_z(1 - 2 * way)
        )

    def start_gz(way, step):
        block = g_held.at[target_of(way, 0)] if step == 0 else g_slots[way].at[step - 1]
        at = (way, step)
        gz[at] = send(
            block, g_slots[way].at[step], (gz_send.at[at], gz_recv.at[at]), along_z(1 - 2 * way)
        )

    def start_gy(slot, source, way):
        gy[slot] = send(
            source, g_y.at[slot], (gy_send.at[slot], gy_recv.at[slot]), along_y(1 - 2 * way)
        )

    low, high = pl.ds(0, half), pl.ds(half, half)
    above, below, across = wrap(y_at + 1, SIDE_Y), wrap(y_at - 1, SIDE_Y), wrap(y_at + 2, SIDE_Y)

    def pass_far():
        for slot, row, first, way in ((0, above, 0, 0), (1, below, half, 1)):
            gy[slot].wait_recv()

            def add_row(place, carry, slot=slot, row=row, first=first):
                g_y[slot, place] = rounded_sum(g_y[slot, place], g_part[row, first + place])
                return carry

            lax.fori_loop(0, half, add_row, 0)
            start_gy(4 + slot, g_y.at[slot], way)

    def close_y():
        for slot in (2, 3, 4, 5):
            gy[slot].wait_recv()

        def add_low(place, carry):
            g_held[place] = rounded_sum(g_part[y_at, place], g_y[4, place], g_y[3, place])
            return carry

        def add_high(place, carry):
            g_held[half + place] = rounded_sum(
                g_part[y_at, half + place], g_y[2, place], g_y[5, place]
            )
            return carry

        lax.fori_loop(0, half, add_low, 0)
        lax.fori_loop(0, half, add_high, 0)
        start_gz(0, 0)
        start_gz(1, 0)

    def step_gz(step):
        for way in range(2):
            if step + 1 < step_counts[way]:
                gz[(way, step)].wait_recv()
                slot = g_slots[way]
                slot[step] = rounded_sum(slot[step], g_held[target_of(way, step + 1)])
                start_gz(way, step + 1)

    for piece in range(PIECES):
        for way in range(2):
            start_mz(way, 0, piece)
    start_gy(0, g_part.at[across, low], 0)
    start_gy(1, g_part.at[across, high], 1)
    start_gy(2, g_part.at[above, high], 0)
    start_gy(3, g_part.at[below, low], 1)
    middle = step_counts[0] // 2
    g_step = 0
    for step in range(step_counts[0] - 1):
        for piece in range(PIECES):
            for way in range(2):
                if step + 1 < step_counts[way]:
                    mz[(way, step, piece)].wait_recv()
                    place = target_of(way, step + 1)

                    def add_own(row, carry, way=way, step=step, place=place):
                        slot = m_slots[way]
                        slot[step, row] = rounded_sum(slot[step, row], m_part[row, place])
                        return carry

                    lax.fori_loop(piece * span, (piece + 1) * span, add_own, 0)
                    start_mz(way, step + 1, piece)
            if step > middle:
                step_gz(g_step)
                g_step += 1
        if step == 1:
            pass_far()
        if step == middle:
            close_y()
    for way in range(2):
        for piece in range(PIECES):
            mz[(way, step_counts[way] - 1, piece)].wait_recv()

    def close_z(row, carry):
        m_held[row] = rounded_sum(
            m_part[row, z_at], m_up[step_counts[0] - 1, row], m_down[step_counts[1] - 1, row]
        )
        return carry

    lax.fori_loop(0, SIDE_Y, close_z, 0)
    far = send(m_held.at[across], m_got.at[0], (my_send.at[0], my_recv.at[0]), along_y(1))
    down = send(m_held.at[below], m_got.at[1], (my_send.at[1], my_recv.at[1]), along_y(-1))
    if g_step < step_counts[0] - 1:
        step_gz(g_step)
        g_step += 1
    far.wait_recv()
    m_got[0] = rounded_sum(m_got[0], m_held[above])
    near = send(m_got.at[0], m_got.at[2], (my_send.at[2], my_recv.at[2]), along_y(1))
    while g_step < step_counts[0] - 1:
        step_gz(g_step)
        g_step += 1
    down.wait_recv()
    near.wait_recv()
    m_sum[...] = rounded_sum(m_held[y_at], m_got[1], m_got[2])
    hand_out(0, m_sum, m_out)
    for way in range(2):
        gz[(way, step_counts[way] - 1)].wait_recv()
    g_sum[...] = rounded_sum(
        g_held[z_at], g_up[step_counts[0] - 1], g_down[step_counts[1] - 1]
    )
    hand_out(1, g_sum, g_out)
    for copy in own_copies:
        copy.wait()
    for copy in swapped:
        copy.wait_recv()
    for group in (mz, gz, gy):
        for copy in group.values():
            copy.wait_send()
    for copy in (far, down, near, *swapped):
        copy.wait_send()


def scatter_sums(m_part, g_part, side_z, dp_count):
    all_rows, columns = m_part.shape
    rows = all_rows // (SIDE_Y * side_z)
    up_steps, down_steps = steps_of(side_z)
    kind = m_part.dtype
    vmem = pl.BlockSpec(memory_space=pltpu.VMEM)
    sem = pltpu.SemaphoreType.DMA
    whole = (SIDE_Y, side_z, rows, columns)
    return pl.pallas_call(
        functools.partial(scatter_kernel, side_z, dp_count),
        out_shape=[jax.ShapeDtypeStruct((rows * dp_count, columns // dp_count), kind)] * 2,
        in_specs=[vmem, vmem],
        out_specs=[vmem, vmem],
        scratch_shapes=[
            pltpu.VMEM((rows, columns), kind),
            pltpu.VMEM((rows, columns), kind),
            pltpu.VMEM((up_steps, SIDE_Y, rows, columns), kind),
            pltpu.VMEM((down_steps, SIDE_Y, rows, columns), kind),
            pltpu.VMEM((SIDE_Y, rows, columns), kind),
            pltpu.VMEM((3, rows, columns), kind),
            pltpu.VMEM((6, side_z // 2, rows, columns), kind),
            pltpu.VMEM((side_z, rows, columns), kind),
            pltpu.VMEM((up_steps, rows, columns), kind),
            pltpu.VMEM((down_steps, rows, columns), kind),
            sem((2, up_steps, PIECES)),
            sem((2, up_steps, PIECES)),
            sem((3,)),
            sem((3,)),
            sem((6,)),
            sem((6,)),
            sem((2, up_steps)),
            sem((2, up_steps)),
            sem((2, dp_count - 1)),
            sem((2, dp_count - 1)),
            sem((2,)),
        ],
        compiler_params=pltpu.CompilerParams(
            collective_id=1, has_side_effects=True, vmem_limit_bytes=24 * 2**20
        ),
        cost_estimate=pl.CostEstimate(
            flops=0, bytes_accessed=200 * 2**20, transcendentals=0
        ),
    )(m_part.reshape(whole), g_part.reshape(whole))


def shards(tokens, cotangent, routes, mix_weights, w_gate, w_up, w_down):
    tok_rows, width_dev = tokens.shape
    picks_per = routes.shape[1]
    dp_count = lax.axis_size("dp")
    owner_count = lax.axis_size("expert")
    hidden = w_gate.shape[2]
    sub_rows = tok_rows // dp_count
    width = width_dev * dp_count
    me_dp = lax.axis_index("dp")
    me_expert = lax.axis_index("expert")

    weights_dev = jnp.concatenate([w_gate[0], w_up[0], w_down[0].T], axis=1)
    weights = lax.all_gather(weights_dev, "dp", axis=0, tiled=True)

    my_routes = lax.dynamic_slice_in_dim(routes, me_dp * sub_rows, sub_rows, 0)
    my_mix = lax.dynamic_slice_in_dim(mix_weights, me_dp * sub_rows, sub_rows, 0)
    extra = jnp.concatenate(
        [my_routes.astype(jnp.bfloat16), *split_three(my_mix)], axis=1
    )
    extra = jnp.pad(extra, ((0, 0), (0, 128 - extra.shape[1])))
    x_rows, c_wide = gather_rows(
        tokens, cotangent, extra, owner_count // SIDE_Y, dp_count
    )
    c_rows = c_wide[:, :width]
    tail = c_wide[:, width : width + 4 * picks_per].astype(jnp.float32)
    tail = tail.reshape(-1, 4, picks_per)
    mix_all = tail[:, 1] + tail[:, 2] + tail[:, 3]
    named = tail[:, 0] == me_expert.astype(jnp.float32)
    weight_row = jnp.sum(jnp.where(named, mix_all, 0.0), axis=1, keepdims=True)

    w_in = weights[:, : 2 * hidden]
    w_out = weights[:, 2 * hidden :]
    pre = contract(x_rows, w_in, 1, 0)
    back_hidden = contract(c_rows, w_out, 1, 0) * weight_row
    gate_in, up_in = pre[:, :hidden], pre[:, hidden:]
    activated, slope_silu = silu_parts(gate_in)
    hidden_mix = (activated * up_in * weight_row).astype(jnp.bfloat16)
    gate_back = (back_hidden * up_in * slope_silu).astype(jnp.bfloat16)
    up_back = (back_hidden * activated).astype(jnp.bfloat16)
    in_back = jnp.concatenate([gate_back, up_back], axis=1)

    mixed_part = contract(hidden_mix, w_out, 1, 1).astype(jnp.bfloat16)
    grad_part = contract(in_back, w_in, 1, 1).astype(jnp.bfloat16)
    in_grad = contract(x_rows, in_back, 0, 0).astype(jnp.bfloat16)
    out_grad = contract(c_rows, hidden_mix, 0, 0).astype(jnp.bfloat16)
    weight_grads = lax.psum_scatter(
        jnp.concatenate([in_grad, out_grad], axis=1), "dp", scatter_dimension=0, tiled=True
    ).astype(jnp.float32)
    mixed, token_grad = scatter_sums(mixed_part, grad_part, owner_count // SIDE_Y, dp_count)
    return (
        mixed,
        token_grad,
        weight_grads[None, :, :hidden],
        weight_grads[None, :, hidden : 2 * hidden],
        weight_grads[:, 2 * hidden :].T[None],
    )


def solution(mesh):
    placed = (
        P("expert", "dp"),
        P("expert", "dp"),
        P("expert", None),
        P("expert", None),
        P("expert", "dp", None),
        P("expert", "dp", None),
        P("expert", None, "dp"),
    )
    return jax.shard_map(
        shards,
        mesh=mesh,
        in_specs=placed,
        out_specs=(
            P("expert", "dp"),
            P("expert", "dp"),
            P("expert", "dp", None),
            P("expert", "dp", None),
            P("expert", None, "dp"),
        ),
        check_vma=False,
    )
```
